32 devices in a mesh: dp: 8 (over z, y), tensor: 4 (over x, core).
Axes of the slice: x: 2, y: 2, z: 4, core: 2. Of those that a mesh axis runs over, the one named last changes fastest.
Arguments:
- latents: bfloat16 [16384, 768], P('dp'), may hold values from -6 to 6
- cond: bfloat16 [64, 768], P('dp'), may hold values from -6 to 6
- ada_weight: bfloat16 [768, 4608], replicated, may hold values from -0.21875 to 0.21875
- ada_bias: bfloat16 [4608], replicated, may hold values from -3 to 3
- qkv_weight: bfloat16 [3, 768, 768], P(None, None, 'tensor'), may hold values from -0.21875 to 0.21875
- qv_bias: bfloat16 [2, 768], P(None, 'tensor'), may hold values from -3 to 3
- proj_weight: bfloat16 [768, 768], P('tensor'), may hold values from -0.875 to 0.875
- proj_bias: bfloat16 [768], replicated, may hold values from -3 to 3
- fc1_weight: bfloat16 [768, 3072], P(None, 'tensor'), may hold values from -0.21875 to 0.21875
- fc1_bias: bfloat16 [3072], P('tensor'), may hold values from -3 to 3
- fc2_weight: bfloat16 [3072, 768], P('tensor'), may hold values from -0.21875 to 0.21875
- fc2_bias: bfloat16 [768], replicated, may hold values from -6 to 6
- cotangent: bfloat16 [16384, 768], P('dp'), may hold values from -0.375 to 0.375
Outputs:
- block_output: float32 [16384, 768], P('dp')
- latents_grad: float32 [16384, 768], P('dp')
- cond_grad: float32 [64, 768], P('dp')
- ada_weight_grad: float32 [768, 4608], P(None, 'tensor')
- ada_bias_grad: float32 [4608], P('tensor')
- qkv_weight_grad: float32 [3, 768, 768], P(None, None, 'tensor')
- qv_bias_grad: float32 [2, 768], P(None, 'tensor')
- proj_weight_grad: float32 [768, 768], P('tensor')
- proj_bias_grad: float32 [768], replicated
- fc1_weight_grad: float32 [768, 3072], P(None, 'tensor')
- fc1_bias_grad: float32 [3072], P('tensor')
- fc2_weight_grad: float32 [3072, 768], P('tensor')
- fc2_bias_grad: float32 [768], replicated
The draws below stay inside these ranges and needn't reach their ends.
All inputs are finite; a program needn't handle non-finite values.
Results may differ from the reference program's by a relative error of at most 0.014.
The reference program's roundings to bfloat16 on the way count: a program that leaves them out, or rounds other values in their place, can miss the bound.
Values sent between devices are 32-bit elements; how exact they have to be, the bound alone decides.
No kernel may reach another device: no remote copies, remote signals or barrier semaphores. Data moves between devices by JAX's collectives and lax.ppermute only.
A program may use at most 256 MiB of HBM per device.

```python
import math
import jax
import jax.numpy as jnp
from jax import lax

D = 768
HEADS = 12
HEAD_DIM = 64
FF = 3072
SEQ = 256
LAT_DEV = 8
LATENTS = 64
TOKENS = 16384


def level_of(key, dims, split, smallest, largest):
    factor_of = 1.0
    for dim, blocks in split:
        draws = jax.random.uniform(jax.random.fold_in(jax.random.fold_in(key, 6), dim), (blocks,), jnp.float32, smallest / len(split), largest / len(split))
        factor_of = factor_of * jnp.repeat(jnp.exp(draws), dims[dim] // blocks).reshape((-1,) + (1,) * (len(dims) - 1 - dim))
    return factor_of


def bell_draw(stream_key, shape, deviation, most, pieces=(), kind=jnp.bfloat16):
    factor_of = level_of(stream_key, shape, pieces, -0.22, 0.18) if pieces else 1.0
    array = jax.random.normal(stream_key, shape, jnp.float32) * deviation * factor_of
    return jnp.minimum(jnp.maximum(array, -most), most).astype(kind)


def setup_inputs(seed: int = 0) -> dict:
    seeds = jax.random.split(jax.random.key(seed), 14)
    latents = bell_draw(seeds[0], (TOKENS, D), 1.0, 6.0, ((0, 8),))
    cond = bell_draw(seeds[1], (LATENTS, D), 1.0, 6.0, ((0, 8),))
    ada_weight = bell_draw(seeds[2], (D, 6 * D), D ** -0.5, 0.21875)
    ada_bias = bell_draw(seeds[3], (6 * D,), 0.5, 3.0)
    qkv_weight = bell_draw(seeds[4], (3, D, D), D ** -0.5, 0.21875, ((2, 4),))
    qv_bias = bell_draw(seeds[5], (2, D), 0.5, 3.0, ((1, 4),))
    proj_weight = bell_draw(seeds[6], (D, D), (D // 16) ** -0.5, 0.875, ((0, 4),))
    proj_bias = bell_draw(seeds[7], (D,), 0.5, 3.0)
    fc1_weight = bell_draw(seeds[8], (D, FF), D ** -0.5, 0.21875, ((1, 4),))
    fc1_bias = bell_draw(seeds[9], (FF,), 0.5, 3.0, ((0, 4),))
    fc2_weight = bell_draw(seeds[10], (FF, D), (FF // 4) ** -0.5, 0.21875, ((0, 4),))
    fc2_bias = bell_draw(seeds[11], (D,), 1.2, 6.0)
    cotangent = bell_draw(seeds[12], (TOKENS, D), 0.0625, 0.375, ((0, 8),))
    return {"latents": latents, "cond": cond, "ada_weight": ada_weight, "ada_bias": ada_bias, "qkv_weight": qkv_weight, "qv_bias": qv_bias, "proj_weight": proj_weight, "proj_bias": proj_bias, "fc1_weight": fc1_weight, "fc1_bias": fc1_bias, "fc2_weight": fc2_weight, "fc2_bias": fc2_bias, "cotangent": cotangent}


EPS = 1e-06
GELU_C = 0.7978845608028654
GELU_A = 0.044715

def half_float(values):
    return lax.optimization_barrier(values.astype(jnp.bfloat16)).astype(jnp.float32)

def layer_stats(values):
    mean = lax.optimization_barrier(jnp.mean(values, axis=-1, keepdims=True))
    centered = values - mean
    variance = lax.optimization_barrier(jnp.mean(centered * centered, axis=-1, keepdims=True))
    inverse = lax.rsqrt(variance + EPS)
    return (centered * inverse, inverse)

def layer_back(grad_norm, normed, inverse):
    first = lax.optimization_barrier(jnp.mean(grad_norm, axis=-1, keepdims=True))
    second = lax.optimization_barrier(jnp.mean(grad_norm * normed, axis=-1, keepdims=True))
    return inverse * (grad_norm - first - normed * second)

def gelu_tanh(values):
    return 0.5 * values * (1.0 + jnp.tanh(GELU_C * (values + GELU_A * values * values * values)))

def gelu_slope(values):
    tangent = jnp.tanh(GELU_C * (values + GELU_A * values * values * values))
    return 0.5 * (1.0 + tangent) + 0.5 * values * (1.0 - tangent * tangent) * GELU_C * (1.0 + 3.0 * GELU_A * values * values)

def run_block(latents, cotangent, cond, ada_weight, ada_bias, qkv_weight, qv_bias, proj_weight, proj_bias, fc1_weight, fc1_bias, fc2_weight, fc2_bias):
    count = cond.shape[0]
    rows = count * SEQ
    scale = 1.0 / math.sqrt(HEAD_DIM)
    cond_float = cond.astype(jnp.float32)
    sigmoid = jax.nn.sigmoid(cond_float)
    activated = (cond_float * sigmoid).astype(jnp.bfloat16)
    modulation = jnp.dot(activated, ada_weight, preferred_element_type=jnp.float32) + ada_bias.astype(jnp.float32)
    vectors = modulation.reshape(count, 6, 1, D)
    shift_one, scale_one, gate_one = (vectors[:, 0], vectors[:, 1], vectors[:, 2])
    shift_two, scale_two, gate_two = (vectors[:, 3], vectors[:, 4], vectors[:, 5])
    inputs = latents.astype(jnp.float32).reshape(count, SEQ, D)
    normed_one, inverse_one = layer_stats(inputs)
    modulated_one = (normed_one * (1.0 + scale_one) + shift_one).astype(jnp.bfloat16).reshape(rows, D)
    query = (jnp.dot(modulated_one, qkv_weight[0], preferred_element_type=jnp.float32) + qv_bias[0].astype(jnp.float32)).astype(jnp.bfloat16)
    keys = jnp.dot(modulated_one, qkv_weight[1], preferred_element_type=jnp.float32).astype(jnp.bfloat16)
    values = (jnp.dot(modulated_one, qkv_weight[2], preferred_element_type=jnp.float32) + qv_bias[1].astype(jnp.float32)).astype(jnp.bfloat16)
    head_shape = (count, SEQ, HEADS, HEAD_DIM)
    query_heads = half_float(query).reshape(head_shape)
    key_heads = half_float(keys).reshape(head_shape)
    value_heads = half_float(values).reshape(head_shape)
    scores = jnp.einsum('bqhd,bkhd->bhqk', query_heads, key_heads) * scale
    top = lax.optimization_barrier(jnp.max(scores, axis=-1, keepdims=True))
    logsum = top + jnp.log(lax.optimization_barrier(jnp.sum(jnp.exp(scores - top), axis=-1, keepdims=True)))
    probs = jnp.exp(scores - logsum)
    probs_half = half_float(probs)
    attended = jnp.einsum('bhqk,bkhd->bqhd', probs_half, value_heads).astype(jnp.bfloat16).reshape(rows, D)
    attention = (jnp.dot(attended, proj_weight, preferred_element_type=jnp.float32) + proj_bias.astype(jnp.float32)).reshape(count, SEQ, D)
    middle = inputs + gate_one * attention
    normed_two, inverse_two = layer_stats(middle)
    modulated_two = (normed_two * (1.0 + scale_two) + shift_two).astype(jnp.bfloat16).reshape(rows, D)
    hidden_pre = jnp.dot(modulated_two, fc1_weight, preferred_element_type=jnp.float32) + fc1_bias.astype(jnp.float32)
    hidden = gelu_tanh(hidden_pre).astype(jnp.bfloat16)
    feedforward = (jnp.dot(hidden, fc2_weight, preferred_element_type=jnp.float32) + fc2_bias.astype(jnp.float32)).reshape(count, SEQ, D)
    block_output = (middle + gate_two * feedforward).reshape(rows, D)
    grad_out = cotangent.astype(jnp.float32).reshape(count, SEQ, D)
    gate_two_grad = lax.optimization_barrier(jnp.sum(grad_out * feedforward, axis=1))
    ff_grad = grad_out * gate_two
    fc2_bias_grad = lax.optimization_barrier(jnp.sum(ff_grad, axis=(0, 1)))
    ff_half = ff_grad.astype(jnp.bfloat16).reshape(rows, D)
    fc2_weight_grad = jnp.dot(hidden.T, ff_half, preferred_element_type=jnp.float32)
    pre_grad = jnp.dot(ff_half, fc2_weight.T, preferred_element_type=jnp.float32) * gelu_slope(hidden_pre)
    fc1_bias_grad = lax.optimization_barrier(jnp.sum(pre_grad, axis=0))
    pre_half = pre_grad.astype(jnp.bfloat16)
    fc1_weight_grad = jnp.dot(modulated_two.T, pre_half, preferred_element_type=jnp.float32)
    mod_two_grad = jnp.dot(pre_half, fc1_weight.T, preferred_element_type=jnp.float32).reshape(count, SEQ, D)
    shift_two_grad = lax.optimization_barrier(jnp.sum(mod_two_grad, axis=1))
    scale_two_grad = lax.optimization_barrier(jnp.sum(mod_two_grad * normed_two, axis=1))
    middle_grad = grad_out + layer_back(mod_two_grad * (1.0 + scale_two), normed_two, inverse_two)
    gate_one_grad = lax.optimization_barrier(jnp.sum(middle_grad * attention, axis=1))
    attention_grad = middle_grad * gate_one
    proj_bias_grad = lax.optimization_barrier(jnp.sum(attention_grad, axis=(0, 1)))
    attention_half = attention_grad.astype(jnp.bfloat16).reshape(rows, D)
    proj_weight_grad = jnp.dot(attended.T, attention_half, preferred_element_type=jnp.float32)
    attended_grad = jnp.dot(attention_half, proj_weight.T, preferred_element_type=jnp.float32).astype(jnp.bfloat16)
    grad_heads = half_float(attended_grad).reshape(head_shape)
    scores_again = jnp.einsum('bqhd,bkhd->bhqk', query_heads, key_heads) * scale
    probs_again = jnp.exp(scores_again - logsum)
    prob_grad = jnp.einsum('bqhd,bkhd->bhqk', grad_heads, value_heads)
    delta = lax.optimization_barrier(jnp.sum(probs_again * prob_grad, axis=-1, keepdims=True))
    score_grad = probs_again * (prob_grad - delta) * scale
    score_half = half_float(score_grad)
    query_grad = jnp.einsum('bhqk,bkhd->bqhd', score_half, key_heads).reshape(rows, D)
    key_grad = jnp.einsum('bhqk,bqhd->bkhd', score_half, query_heads).reshape(rows, D)
    value_grad = jnp.einsum('bhqk,bqhd->bkhd', half_float(probs_again), grad_heads).reshape(rows, D)
    qv_bias_grad = jnp.stack([lax.optimization_barrier(jnp.sum(query_grad, axis=0)), lax.optimization_barrier(jnp.sum(value_grad, axis=0))])
    stacked_half = jnp.stack([query_grad, key_grad, value_grad]).astype(jnp.bfloat16)
    qkv_weight_grad = jnp.stack([jnp.dot(modulated_one.T, stacked_half[index], preferred_element_type=jnp.float32) for index in range(3)])
    mod_one_grad = jnp.einsum('srd,sed->re', half_float(stacked_half), qkv_weight.astype(jnp.float32)).reshape(count, SEQ, D)
    shift_one_grad = lax.optimization_barrier(jnp.sum(mod_one_grad, axis=1))
    scale_one_grad = lax.optimization_barrier(jnp.sum(mod_one_grad * normed_one, axis=1))
    input_grad = middle_grad + layer_back(mod_one_grad * (1.0 + scale_one), normed_one, inverse_one)
    latents_grad = input_grad.reshape(rows, D)
    modulation_grad = jnp.stack([shift_one_grad, scale_one_grad, gate_one_grad, shift_two_grad, scale_two_grad, gate_two_grad], axis=1).reshape(count, 6 * D)
    ada_weight_grad = jnp.dot(activated.astype(jnp.float32).T, modulation_grad, precision=lax.Precision.HIGHEST)
    ada_bias_grad = lax.optimization_barrier(jnp.sum(modulation_grad, axis=0))
    activated_grad = jnp.dot(modulation_grad, ada_weight.astype(jnp.float32).T, precision=lax.Precision.HIGHEST)
    cond_grad = activated_grad * sigmoid * (1.0 + cond_float * (1.0 - sigmoid))
    return (block_output, latents_grad, cond_grad, ada_weight_grad, ada_bias_grad, qkv_weight_grad, qv_bias_grad, proj_weight_grad, proj_bias_grad, fc1_weight_grad, fc1_bias_grad, fc2_weight_grad, fc2_bias_grad)

def reference(latents, cond, ada_weight, ada_bias, qkv_weight, qv_bias, proj_weight, proj_bias, fc1_weight, fc1_bias, fc2_weight, fc2_bias, cotangent):
    blocks = LATENTS // LAT_DEV
    latent_blocks = latents.reshape(blocks, LAT_DEV * SEQ, D)
    cotangent_blocks = cotangent.reshape(blocks, LAT_DEV * SEQ, D)
    cond_blocks = cond.reshape(blocks, LAT_DEV, D)
    weights = (ada_weight, ada_bias, qkv_weight, qv_bias, proj_weight, proj_bias, fc1_weight, fc1_bias, fc2_weight, fc2_bias)
    initial = tuple((jnp.zeros(weight.shape, jnp.float32) for weight in weights))

    def visit(carry, inputs):
        latent_block, cotangent_block, cond_block = inputs
        results = run_block(latent_block, cotangent_block, cond_block, *weights)
        totals = tuple((before + after for before, after in zip(carry, results[3:])))
        return (totals, (results[0], results[1], results[2]))
    totals, (outputs, input_grads, cond_grads) = lax.scan(visit, initial, (latent_blocks, cotangent_blocks, cond_blocks))
    return (outputs.reshape(TOKENS, D), input_grads.reshape(TOKENS, D), cond_grads.reshape(LATENTS, D), totals[0], totals[1], totals[2], totals[3], totals[4], totals[5], totals[6], totals[7], totals[8], totals[9])
```

```python
import functools
import math

import jax
import jax.numpy as jnp
from jax import lax
from jax.experimental import pallas as pl
from jax.experimental.pallas import tpu as pltpu
from jax.sharding import PartitionSpec as P

HEAD_DIM = 64
SEQ = 256
EPS = 1e-06
GELU_C = 0.7978845608028654
GELU_A = 0.044715
F32 = jnp.float32
BF16 = jnp.bfloat16


def layer_stats(values):
    mean = jnp.mean(values, axis=-1, keepdims=True)
    centered = values - mean
    variance = jnp.mean(centered * centered, axis=-1, keepdims=True)
    inverse = lax.rsqrt(variance + EPS)
    return (centered * inverse, inverse)


def layer_back(grad_norm, normed, inverse):
    first = jnp.mean(grad_norm, axis=-1, keepdims=True)
    second = jnp.mean(grad_norm * normed, axis=-1, keepdims=True)
    return inverse * (grad_norm - first - normed * second)


def gelu_pair(values):
    square = values * values
    tangent = jnp.tanh(GELU_C * (values + GELU_A * values * square))
    ramp = 0.5 * (1.0 + tangent)
    slope = ramp + 0.5 * values * (1.0 - tangent * tangent) * (GELU_C * (1.0 + 3.0 * GELU_A * square))
    return values * ramp, slope


def mm(a, b):
    return jnp.dot(a, b, preferred_element_type=F32)


def mm_nt(a, b):
    return lax.dot_general(a, b, (((1,), (1,)), ((), ())), preferred_element_type=F32)


def mm_tn(a, b):
    return lax.dot_general(a, b, (((0,), (0,)), ((), ())), preferred_element_type=F32)


def col_sum(a):
    return jnp.sum(a, axis=0, keepdims=True)


def head_pair(ref, pair):
    both = ref[:, pair * 128 : pair * 128 + 128]
    low = lax.broadcasted_iota(jnp.int32, both.shape, 1) < HEAD_DIM
    zero = jnp.zeros_like(both)
    return both, (jnp.where(low, both, zero), jnp.where(low, zero, both))


def half_body(x_ref, o_ref):
    o_ref[...] = x_ref[...].astype(BF16)


def half(a):
    tile = a.shape[0] // 4 if a.shape[0] % 64 == 0 else a.shape[0]
    spec = pl.BlockSpec((tile, a.shape[1]), lambda i: (i, 0))
    return pl.pallas_call(
        half_body, grid=(a.shape[0] // tile,), in_specs=[spec], out_specs=spec,
        out_shape=jax.ShapeDtypeStruct(a.shape, BF16), name="half",
    )(a)


def load_weights(first, second, w_ref, local):
    for part in range(4):
        rows = slice(part * local, part * local + local)
        w_ref[part, :local] = first[rows].astype(BF16)
        w_ref[part, local:] = second[rows].astype(BF16)


def attend(mod, w_ref, bias_q, bias_v, q_ref, k_ref, v_ref, a_ref, ls_ref):
    scale = 1.0 / math.sqrt(HEAD_DIM)
    q_ref[...] = (mm_nt(mod, w_ref[0]) + bias_q).astype(BF16)
    k_ref[...] = mm_nt(mod, w_ref[1]).astype(BF16)
    v_ref[...] = (mm_nt(mod, w_ref[2]) + bias_v).astype(BF16)
    for pair in range(q_ref.shape[1] // 128):
        _, queries = head_pair(q_ref, pair)
        keys, _ = head_pair(k_ref, pair)
        _, values = head_pair(v_ref, pair)
        total = 0.0
        for head in range(2):
            scores = mm_nt(queries[head], keys) * scale
            top = jnp.max(scores, axis=-1, keepdims=True)
            logsum = top + jnp.log(jnp.sum(jnp.exp(scores - top), axis=-1, keepdims=True))
            column = pair * 2 + head
            ls_ref[:, column : column + 1] = logsum
            total = total + mm(jnp.exp(scores - logsum).astype(BF16), values[head])
        a_ref[:, pair * 128 : pair * 128 + 128] = total.astype(BF16)
    return mm(a_ref[...], w_ref[3])


def front_body(
    s_ref, lat_ref, vec_ref, w0_ref, w1_ref, mod_ref, q_ref, k_ref, v_ref, a_ref, ls_ref, part_ref, w_ref, *, local
):
    @pl.when(pl.program_id(0) == 0)
    def _():
        load_weights(w0_ref, w1_ref, w_ref, local)

    normed, _ = layer_stats(lat_ref[...].astype(F32))
    mod = (normed * (1.0 + vec_ref[0, 1:2]) + vec_ref[0, 0:1]).astype(BF16)
    mod_ref[...] = mod
    row, wide = 4 * local, 2 * local
    bias_q = w0_ref[row : row + 1, :wide] + w1_ref[row + 1 : row + 2, :wide]
    bias_v = w0_ref[row + 2 : row + 3, :wide] + w1_ref[row + 3 : row + 4, :wide]
    part_ref[...] = attend(mod, w_ref, bias_q, bias_v, q_ref, k_ref, v_ref, a_ref, ls_ref)


def middle_body(
    s_ref, lat_ref, vec_ref, w0_ref, w1_ref, mod_ref, part_ref, pb_ref, *rest, local, first
):
    outs = rest[-9:-1] if first else rest[-8:]
    q_ref, k_ref, v_ref, a_ref, ls_ref, att_ref, mod2_ref, send_ref = outs
    row, wide = (4 * local if first else 0), 2 * local
    if first:
        w_ref = rest[-1]
        load_weights(w0_ref, w1_ref, w_ref, local)
    else:
        w_ref = rest[0]
    bias_q = w0_ref[row : row + 1, :wide] + w1_ref[row + 1 : row + 2, :wide]
    bias_v = w0_ref[row + 2 : row + 3, :wide] + w1_ref[row + 3 : row + 4, :wide]
    share = attend(mod_ref[...], w_ref, bias_q, bias_v, q_ref, k_ref, v_ref, a_ref, ls_ref)
    attention = part_ref[...] + share + pb_ref[...].astype(F32)
    att_ref[...] = attention
    middle = lat_ref[...].astype(F32) + vec_ref[0, 2:3] * attention
    normed, _ = layer_stats(middle)
    mod = (normed * (1.0 + vec_ref[0, 4:5]) + vec_ref[0, 3:4]).astype(BF16)
    mod2_ref[...] = mod
    send_ref[...] = mod.astype(F32)


def mlp_body(s_ref, x_ref, g_ref, vec_ref, w1o_ref, w2o_ref, b1_ref, wc_ref, *rest):
    xh_ref, ho_ref, hc_ref, po_ref, pc_ref, fh_ref, back_ref, ff_ref, bs_ref = rest[-9:]
    width = x_ref.shape[1]
    hid = w1o_ref.shape[1]

    @pl.when(pl.program_id(0) == 0)
    def _():
        bs_ref[...] = jnp.zeros_like(bs_ref)

    x = x_ref[...].astype(BF16)
    xh_ref[...] = x
    ff_half = (g_ref[...].astype(F32) * vec_ref[0, 5:6]).astype(BF16)
    fh_ref[...] = ff_half
    for part in range(2):
        w1 = w1o_ref[...] if part == 0 else wc_ref[:width]
        w2 = w2o_ref[...] if part == 0 else wc_ref[width : width + hid]
        bias = b1_ref[...].astype(F32) if part == 0 else wc_ref[width + hid : width + hid + 1].astype(F32)
        hidden, slope = gelu_pair(mm(x, w1) + bias)
        hidden = hidden.astype(BF16)
        (ho_ref, hc_ref)[part][...] = hidden
        pre = mm_nt(ff_half, w2) * slope
        bs_ref[part : part + 1] += col_sum(pre)
        pre = pre.astype(BF16)
        (po_ref, pc_ref)[part][...] = pre
        if part == 0:
            back_ref[...] = mm_nt(pre, w1)
            ff_ref[...] = mm(hidden, w2)
        else:
            back_ref[...] += mm_nt(pre, w1)
            ff_ref[...] += mm(hidden, w2)


def back_body(
    s_ref, lat_ref, vec_ref, g_ref, att_ref, b0_ref, b1_ref, qa_ref, ka_ref, va_ref, aa_ref, la_ref,
    qb_ref, kb_ref, vb_ref, ab_ref, lb_ref, wa_ref, wb_ref, *rest
):
    lhs_ref, ah_ref, grad_ref, sums_ref, mid_ref, go_ref, d_ref = rest[-7:]
    scale = 1.0 / math.sqrt(HEAD_DIM)
    wide = qa_ref.shape[1]
    inputs = lat_ref[...].astype(F32)
    attention = att_ref[...]
    normed, inverse = layer_stats(inputs + vec_ref[0, 2:3] * attention)
    grad = b0_ref[...] + b1_ref[...]
    sums_ref[0, 3:4] = col_sum(grad)
    sums_ref[0, 4:5] = col_sum(grad * normed)
    middle_grad = g_ref[...].astype(F32) + layer_back(grad * (1.0 + vec_ref[0, 4:5]), normed, inverse)
    mid_ref[...] = middle_grad
    sums_ref[0, 2:3] = col_sum(middle_grad * attention)
    att_grad = middle_grad * vec_ref[0, 2:3]
    sums_ref[0, 6:7] = col_sum(att_grad)
    ah = att_grad.astype(BF16)
    ah_ref[...] = ah
    go_ref[:, :wide] = mm_nt(ah, wa_ref[3]).astype(BF16)
    go_ref[:, wide:] = mm_nt(ah, wb_ref[3]).astype(BF16)
    lhs_ref[3, :, :wide] = aa_ref[...]
    lhs_ref[3, :, wide:] = ab_ref[...]
    pairs = wide // 128
    for side in range(2):
        q_ref, k_ref, v_ref, l_ref = ((qa_ref, ka_ref, va_ref, la_ref), (qb_ref, kb_ref, vb_ref, lb_ref))[side]
        for pair in range(pairs):
            _, queries = head_pair(q_ref, pair)
            key_both, keys = head_pair(k_ref, pair)
            value_both, _ = head_pair(v_ref, pair)
            _, grads = head_pair(go_ref, side * pairs + pair)
            dq, dk, dv = 0.0, 0.0, 0.0
            for head in range(2):
                column = pair * 2 + head
                probs = jnp.exp(mm_nt(queries[head], key_both) * scale - l_ref[:, column : column + 1])
                prob_grad = mm_nt(grads[head], value_both)
                delta = jnp.sum(probs * prob_grad, axis=-1, keepdims=True)
                score = (probs * (prob_grad - delta) * scale).astype(BF16)
                dq = dq + mm(score, keys[head])
                dk = dk + mm_tn(score, queries[head])
                dv = dv + mm_tn(probs.astype(BF16), grads[head])
            at = side * wide + pair * 128
            sums_ref[0, 7:8, at : at + 128] = col_sum(dq)
            sums_ref[0, 8:9, at : at + 128] = col_sum(dv)
            lhs_ref[0, :, at : at + 128] = dq.astype(BF16)
            lhs_ref[1, :, at : at + 128] = dk.astype(BF16)
            lhs_ref[2, :, at : at + 128] = dv.astype(BF16)
    for part in range(3):
        share = mm(lhs_ref[part, :, :wide], wa_ref[part]) + mm(lhs_ref[part, :, wide:], wb_ref[part])
        if part == 0:
            d_ref[...] = share
        else:
            d_ref[...] += share
    grad = d_ref[...]
    normed, inverse = layer_stats(inputs)
    sums_ref[0, 0:1] = col_sum(grad)
    sums_ref[0, 1:2] = col_sum(grad * normed)
    grad_ref[...] = mid_ref[...] + layer_back(grad * (1.0 + vec_ref[0, 1:2]), normed, inverse)


def grads_body(lhs_ref, rhs_ref, o_ref):
    out = mm_tn(lhs_ref[0], rhs_ref[0])
    rows = o_ref.shape[2]
    for group in range(o_ref.shape[0]):
        o_ref[group, 0] = out[group * rows : group * rows + rows]


def add_split(parts, index, count, name):
    rows, width = parts[0].shape
    piece = rows // count
    tile = piece
    while tile * width * 4 * count > (2 << 20) and tile % 16 == 0:
        tile //= 2
    steps = piece // tile
    n = len(parts)

    def body(s_ref, *refs):
        for j in range(count):
            total = refs[j * n][...]
            for p in range(1, n):
                total = total + refs[j * n + p][...]
            refs[count * n + j][...] = total

    def in_spec(j):
        return pl.BlockSpec((tile, width), lambda i, s: (s[j] * steps + i, 0))

    return pl.pallas_call(
        body,
        grid_spec=pltpu.PrefetchScalarGridSpec(
            num_scalar_prefetch=1, grid=(steps,),
            in_specs=[in_spec(j) for j in range(count) for _ in range(n)],
            out_specs=[pl.BlockSpec((tile, width), lambda i, s: (i, 0))] * count,
        ),
        out_shape=[jax.ShapeDtypeStruct((piece, width), F32)] * count,
        name=name,
    )(index, *[p for _ in range(count) for p in parts])


def solution(mesh):
    tensor = mesh.shape["tensor"]
    dp = mesh.shape["dp"]
    ring = dp // 2
    assert tensor == 4 and dp % 2 == 0

    def px(a):
        return lax.ppermute(a, "tensor", [(i, i ^ 2) for i in range(tensor)])

    def pc(a):
        return lax.ppermute(a, "tensor", [(i, i ^ 1) for i in range(tensor)])

    def py(a):
        return lax.ppermute(a, "dp", [(i, i ^ 1) for i in range(dp)])

    def pz(a, k):
        return lax.ppermute(
            a, "dp", [(i, ((i >> 1) + k) % ring * 2 + (i & 1)) for i in range(dp)]
        )

    def gather_dp(a):
        pair = jnp.stack([a, py(a)])
        return jnp.stack([pair] + [pz(pair, k) for k in range(1, ring)])

    def reduce_dp(parts, d, name):
        y, z = d & 1, d >> 1
        kept, sent = add_split(parts, jnp.stack([y, 1 - y]), 2, name + "_y")
        got = py(sent)
        pieces = add_split(
            [kept, got], jnp.stack([(z + k) % ring for k in range(ring)]), ring, name + "_z"
        )
        own = pieces[0]
        for k in range(1, ring):
            own = own + pz(pieces[k], k)
        piece, width = own.shape
        full = jnp.zeros((ring * piece, width), F32)
        full = lax.dynamic_update_slice_in_dim(full, own, z * piece, 0)
        for k in range(1, ring):
            full = lax.dynamic_update_slice_in_dim(full, pz(own, k), (z - k) % ring * piece, 0)
        other = py(full)
        out = jnp.zeros((2, ring * piece, width), F32)
        out = lax.dynamic_update_slice_in_dim(out, full[None], y, 0)
        out = lax.dynamic_update_slice_in_dim(out, other[None], 1 - y, 0)
        return out.reshape(2 * ring * piece, width)

    def spread(own, t):
        pair = jnp.stack([own, px(own)])
        cross = pc(pair)
        out = jnp.zeros((tensor,) + own.shape, own.dtype)
        for i, block in ((0, pair[0]), (2, pair[1]), (1, cross[0]), (3, cross[1])):
            out = lax.dynamic_update_slice_in_dim(out, block[None], t ^ i, 0)
        return out.reshape((tensor * own.shape[0],) + own.shape[1:])

    def on_device(
        latents, cond, ada_weight, ada_bias, qkv_weight, qv_bias, proj_weight, proj_bias,
        fc1_weight, fc1_bias, fc2_weight, fc2_bias, cotangent,
    ):
        t = lax.axis_index("tensor")
        d = lax.axis_index("dp")
        count, width = cond.shape
        rows = latents.shape[0] // tensor
        lats = count // tensor
        local = qkv_weight.shape[2]
        wide = 2 * local
        hid = fc1_weight.shape[1]
        base = jnp.stack([t * lats, (t ^ 2) * lats]).astype(jnp.int32)

        def block(a, i):
            size = a.shape[0] // tensor
            return lax.dynamic_slice_in_dim(a, i * size, size, 0)

        def struct(*shape, dtype=F32):
            return jax.ShapeDtypeStruct(shape, dtype)

        anywhere = pl.BlockSpec(memory_space=pl.ANY)

        def whole(a):
            nd = a.ndim
            return pl.BlockSpec(a.shape, lambda i, s: (0,) * nd, pipeline_mode=pl.Buffered(1))

        def at(row, side=0):
            return pl.BlockSpec((SEQ, width), lambda i, s: (s[side] + row + i, 0))

        def vec_at(row, side=0):
            return pl.BlockSpec((1, 6, width), lambda i, s: (s[side] + row + i, 0, 0))

        def seq(cols, row=0):
            return pl.BlockSpec((SEQ, cols), lambda i, s: (row + i, 0))

        def call(body, grid, in_specs, out_specs, out_shape, args, name, aliases=None, scratch=()):
            return pl.pallas_call(
                body,
                grid_spec=pltpu.PrefetchScalarGridSpec(
                    num_scalar_prefetch=1, grid=(grid,), in_specs=in_specs, out_specs=out_specs,
                    scratch_shapes=list(scratch),
                ),
                out_shape=out_shape, input_output_aliases=aliases or {}, name=name,
            )(base, *args)

        bias_row = qv_bias.astype(F32)
        zeros = jnp.zeros((local,), F32)
        tail = jnp.zeros((width - wide,), F32)
        att_own = jnp.concatenate(
            [
                qkv_weight.transpose(0, 2, 1).reshape(3 * local, width).astype(F32),
                proj_weight.astype(F32),
                jnp.concatenate([bias_row[0], zeros, tail])[None],
                jnp.concatenate([zeros, bias_row[0], tail])[None],
                jnp.concatenate([bias_row[1], zeros, tail])[None],
                jnp.concatenate([zeros, bias_row[1], tail])[None],
                jnp.zeros((4, width), F32),
            ],
            0,
        )
        att_x = px(att_own)
        att_c = pc(att_own)
        att_d = pc(att_x)
        ff_own = jnp.concatenate(
            [fc1_weight.astype(F32), fc2_weight.astype(F32), jnp.pad(fc1_bias.astype(F32)[None], ((0, 7), (0, 0)))], 0
        )
        ff_c = half(pc(ff_own))

        cond_float = cond.astype(F32)
        sigmoid = jax.nn.sigmoid(cond_float)
        activated = (cond_float * sigmoid).astype(BF16)
        modulation = mm(activated, ada_weight) + ada_bias.astype(F32)
        vectors = modulation.reshape(count, 6, width)

        head_shapes = [struct(rows, wide, dtype=BF16)] * 4 + [struct(rows, 128)]
        mod_one, qa, ka, va, aa, la, part, wa = call(
            functools.partial(front_body, local=local), lats,
            [at(0), vec_at(0), whole(att_own), whole(att_c)],
            [seq(width)] + [seq(wide)] * 4 + [seq(128), seq(width),
             pl.BlockSpec((4, wide, width), lambda i, s: (0, 0, 0))],
            [struct(rows, width, dtype=BF16)] + head_shapes + [struct(rows, width), struct(4, wide, width, dtype=BF16)],
            (latents, vectors, att_own, att_c), "front",
        )
        mid_shapes = head_shapes + [struct(rows, width), struct(rows, width, dtype=BF16)]
        proj_row = proj_bias[None]
        held, sends, wb = None, [], None
        for lat in range(lats):
            first = lat == 0
            tails = (att_x, att_d) if first else (att_x[4 * local :], att_d[4 * local :])
            args = [latents, vectors, *tails, mod_one, part, proj_row]
            specs = [at(lat), vec_at(lat), whole(tails[0]), whole(tails[1]), seq(width, lat), seq(width, lat), whole(proj_row)]
            aliases = {}
            if not first:
                args.append(wb)
                specs.append(whole(wb))
                aliases = {len(args) + 1 + i: i for i in range(len(held))}
                args += held
                specs += [anywhere] * len(held)
            outs = call(
                functools.partial(middle_body, local=local, first=first), 1, specs,
                [seq(wide, lat)] * 4 + [seq(128, lat), seq(width, lat), seq(width, lat), seq(width)]
                + ([pl.BlockSpec((4, wide, width), lambda i, s: (0, 0, 0))] if first else []),
                mid_shapes + [struct(SEQ, width)] + ([struct(4, wide, width, dtype=BF16)] if first else []),
                args, "middle", aliases,
            )
            held = list(outs[:7])
            sends.append(outs[7])
            if first:
                wb = outs[8]
        qb, kb, vb, ab, lb, attention, mod_two = held
        mod_x = [px(a) for a in sends]

        b1_row = fc1_bias[None]
        mlp_weights = (fc1_weight, fc2_weight, b1_row, ff_c)
        held, backs, ffs, sums = None, [], [], []
        wide_shapes = [struct(2 * rows, width, dtype=BF16)] + [struct(2 * rows, hid, dtype=BF16)] * 4 + [struct(2 * rows, width, dtype=BF16)]
        for step in range(1 + lats):
            grid = lats if step == 0 else 1
            row = 0 if step == 0 else lats + step - 1
            lat, side = (0, 0) if step == 0 else (step - 1, 1)
            x = mod_two if step == 0 else mod_x[step - 1]
            args = [x, cotangent, vectors, *mlp_weights]
            specs = [seq(width), at(lat, side), vec_at(lat, side)] + [whole(a) for a in mlp_weights]
            aliases = {}
            if step:
                aliases = {len(args) + 1 + i: i for i in range(len(held))}
                args += held
                specs += [anywhere] * len(held)
            outs = call(
                mlp_body, grid, specs,
                [seq(width, row)] + [seq(hid, row)] * 4 + [seq(width, row), seq(width), seq(width),
                 pl.BlockSpec((8, hid), lambda i, s: (0, 0))],
                wide_shapes + [struct(grid * SEQ, width)] * 2 + [struct(8, hid)],
                args, "mlp", aliases,
            )
            held = list(outs[:6])
            backs.append(outs[6])
            ffs.append(outs[7])
            sums.append(outs[8])
        mod_all, hid_o, hid_c, pre_o, pre_c, ff_half = held
        fc1_sums = sum(sums[1:], sums[0])
        backs_x = [px(a) for a in backs[1:]]
        ffs_x = [px(a) for a in ffs[1:]]

        got_1 = pc(mm_tn(mod_all, pre_c))
        got_2 = pc(mm_tn(hid_c, ff_half))
        fc2_weight_grad = reduce_dp([mm_tn(hid_o, ff_half), got_2], d, "fc2")
        fc1_weight_grad = reduce_dp([mm_tn(mod_all, pre_o), got_1], d, "fc1")

        held, grads, sums = None, [], []
        for lat in range(lats):
            args = [latents, vectors, cotangent, attention, backs[0], backs_x[lat],
                    qa, ka, va, aa, la, qb, kb, vb, ab, lb, wa, wb]
            specs = [at(lat), vec_at(lat), at(lat), seq(width, lat), seq(width, lat), seq(width)]
            specs += ([seq(wide, lat)] * 4 + [seq(128, lat)]) * 2 + [whole(wa), whole(wb)]
            aliases = {}
            if lat:
                aliases = {len(args) + 1 + i: i for i in range(len(held))}
                args += held
                specs += [anywhere] * len(held)
            outs = call(
                back_body, 1, specs,
                [pl.BlockSpec((4, SEQ, width), lambda i, s, lat=lat: (0, lat, 0)), seq(width, lat), seq(width, lat),
                 pl.BlockSpec((1, 16, width), lambda i, s: (0, 0, 0))],
                [struct(4, rows, width, dtype=BF16), struct(rows, width, dtype=BF16), struct(rows, width),
                 struct(1, 16, width)],
                args, "back", aliases,
                scratch=[pltpu.VMEM((SEQ, width), F32), pltpu.VMEM((SEQ, width), BF16), pltpu.VMEM((SEQ, width), F32)],
            )
            held = list(outs[:3])
            sums.append(outs[3][0])
        lhs, att_half, input_grad = held
        rhs = jnp.stack([mod_one, att_half])
        groups = tensor
        att_grad = pl.pallas_call(
            grads_body, grid=(4,),
            in_specs=[pl.BlockSpec((1, rows, width), lambda i: (i, 0, 0)),
                      pl.BlockSpec((1, rows, width), lambda i: (i // 3, 0, 0))],
            out_specs=pl.BlockSpec((groups, 1, local, width), lambda i: (0, i, 0, 0)),
            out_shape=struct(groups, 4, local, width), name="att_grads",
        )(lhs, rhs).reshape(groups, 4 * local, width)
        att_pair = pc(att_grad[1::2])
        att_sum_x = px(att_grad[2] + att_pair[1])
        att_sum = reduce_dp([att_grad[0], att_pair[0], att_sum_x], d, "att")
        qkv_weight_grad = att_sum[: 3 * local].reshape(3, local, width).transpose(0, 2, 1)
        proj_weight_grad = att_sum[3 * local :]
        latents_grad = spread(input_grad, t)

        own_vec = block(vectors, t)
        gate_one, gate_two = own_vec[:, 2:3], own_vec[:, 5:6]
        inputs = block(latents, t).astype(F32).reshape(lats, SEQ, width)
        grad_own = block(cotangent, t).astype(F32).reshape(lats, SEQ, width)
        middle = inputs + gate_one * attention.reshape(lats, SEQ, width)
        feedforward = ffs[0].reshape(lats, SEQ, width) + jnp.stack(ffs_x) + fc2_bias.astype(F32)
        block_output = spread((middle + gate_two * feedforward).reshape(rows, width), t)
        gate_two_grad = jnp.sum(grad_own * feedforward, axis=1)
        fc2_bias_grad = jnp.sum(grad_own * gate_two, axis=(0, 1))

        shared = sum(sums[1:], sums[0])
        pieces = jnp.concatenate(
            [shared[7].reshape(4, local), shared[8].reshape(4, local), jnp.zeros((4, width - 2 * local), F32)], 1
        )
        small = jnp.concatenate([pieces, shared[6:7], fc2_bias_grad[None], fc1_sums[:2]], 0)
        got = pc(small)
        qv_own = small[0] + got[1]
        qv_x = small[2] + got[3]
        both = small[4:6] + got[4:6]
        fc1_b = small[6] + got[7]
        got = px(jnp.concatenate([qv_x[None], both], 0))
        small = jnp.concatenate([(qv_own + got[0])[None], both + got[1:3], fc1_b[None]], 0)
        small = jnp.sum(gather_dp(small), axis=(0, 1))
        qv_bias_grad = small[0, : 2 * local].reshape(2, local)
        proj_bias_grad = small[1]
        fc2_bias_grad = small[2]
        fc1_bias_grad = small[3]

        modulation_grad = jnp.concatenate([jnp.stack(sums)[:, :5], gate_two_grad[:, None]], 1).reshape(lats, 6 * width)
        modulation_grad = spread(modulation_grad, t)
        share = 6 * width // tensor
        own_grad = lax.dynamic_slice_in_dim(modulation_grad, t * share, share, 1)
        all_grad = gather_dp(own_grad).reshape(dp * count, share)
        all_act = gather_dp(activated.astype(F32)).reshape(dp * count, width)
        ada_weight_grad = lax.dot_general(
            all_act, all_grad, (((0,), (0,)), ((), ())), precision=lax.Precision.HIGHEST, preferred_element_type=F32
        )
        ada_bias_grad = jnp.sum(all_grad, axis=0)
        activated_grad = jnp.dot(modulation_grad, ada_weight.astype(F32).T, precision=lax.Precision.HIGHEST)
        cond_grad = activated_grad * sigmoid * (1.0 + cond_float * (1.0 - sigmoid))
        return (
            block_output, latents_grad, cond_grad, ada_weight_grad, ada_bias_grad, qkv_weight_grad, qv_bias_grad,
            proj_weight_grad, proj_bias_grad, fc1_weight_grad, fc1_bias_grad, fc2_weight_grad, fc2_bias_grad,
        )

    return jax.shard_map(
        on_device,
        mesh=mesh,
        in_specs=(
            P("dp", None), P("dp", None), P(), P(), P(None, None, "tensor"), P(None, "tensor"), P("tensor", None), P(),
            P(None, "tensor"), P("tensor"), P("tensor", None), P(), P("dp", None),
        ),
        out_specs=(
            P("dp", None), P("dp", None), P("dp", None), P(None, "tensor"), P("tensor"), P(None, None, "tensor"),
            P(None, "tensor"), P("tensor", None), P(), P(None, "tensor"), P("tensor"), P("tensor", None), P(),
        ),
        check_vma=False,
    )
```
